512 devices in a mesh: row: 64 (over y_lo, z, x), col: 8 (over y_hi, core).
Axes of the slice: x: 4, y: 8 (y_hi: 4, y_lo: 2; y = y_hi * 2 + y_lo), z: 8, core: 2. Of those that a mesh axis runs over, the one named last changes fastest.
Arguments:
- orbitals: bfloat16 [16384, 2, 256], P(('row', 'col')), may hold values from -6 to 6
- kernel: bfloat16 [16384, 16384], P('row', 'col'), may hold values from -0.0029296875 to 0.0029296875
- basis: bfloat16 [16384, 2048], P('row'), may hold values from -0.046875 to 0.046875
Outputs:
- exchange: float32 [2048, 2, 256], P('row')
The draws below stay inside these ranges and needn't reach their ends.
All inputs are finite; a program needn't handle non-finite values.
Results may differ from the reference program's by a relative error of at most 0.0041.
Values may be sent and summed in bfloat16 or wider, within the bound.
A program may use at most 64 MiB of HBM per device.

```python
import jax
import jax.numpy as jnp
from jax import lax

NOCC = 256
NBASIS = 2048
PR = 256
PIECE = 32
NPTS = 16384
N_ROW = 64
N_COL = 8


def level_of(stream_key, shape, split, least, largest):
    gain = 1.0
    for position, parts in split:
        heights = jax.random.uniform(jax.random.fold_in(jax.random.fold_in(stream_key, 6), position), (parts,), jnp.float32, least / len(split), largest / len(split))
        gain = gain * jnp.repeat(jnp.exp(heights), shape[position] // parts).reshape((-1,) + (1,) * (len(shape) - 1 - position))
    return gain


def scatter_about(rng, extent, spread, bound, shards=(), dtype=jnp.bfloat16):
    values = spread * jax.random.normal(rng, extent, jnp.float32)
    if shards:
        values = values * level_of(rng, extent, shards, -0.22, 0.18)
    return jnp.clip(values, -bound, bound).astype(dtype)


def setup_inputs(seed: int = 0) -> dict:
    key_list = jax.random.split(jax.random.key(seed), 4)
    return {
        "orbitals": scatter_about(key_list[0], (NPTS, 2, NOCC), 1.0, 6.0, ((0, 512),)),
        "kernel": scatter_about(key_list[1], (NPTS, NPTS), (NOCC * NPTS) ** -0.5, 0.0029296875, ((0, 64), (1, 8))),
        "basis": scatter_about(key_list[2], (NPTS, NBASIS), NPTS ** -0.5, 0.046875, ((0, 64),)),
    }


def reference(orbitals, kernel, basis):
    values = orbitals.astype(jnp.float32)
    columns = values.reshape(N_ROW, N_COL, PIECE, 2, NOCC).transpose(1, 0, 2, 3, 4).reshape(NPTS, 2, NOCC)
    row_blocks = values.reshape(N_ROW, PR, 2, NOCC)
    kernel_blocks = kernel.reshape(N_ROW, PR, NPTS)

    def block(block_pair):
        row_values, kernel_rows = block_pair
        density = jnp.einsum("psi,qsi->spq", row_values, columns)
        weighted = (density * kernel_rows.astype(jnp.float32)[None]).astype(jnp.bfloat16)
        weighted = lax.optimization_barrier(weighted).astype(jnp.float32)
        return jnp.einsum("spq,qsi->psi", weighted, columns)

    applied = lax.map(block, (row_blocks, kernel_blocks)).reshape(NPTS, 2, NOCC)
    rounded = lax.optimization_barrier(applied.astype(jnp.bfloat16)).astype(jnp.float32)
    return jnp.einsum("pm,psi->msi", basis.astype(jnp.float32), rounded)
```

```python
import jax
import jax.numpy as jnp
from jax import lax
from jax.experimental import pallas as pl
from jax.experimental.pallas import tpu as pltpu
from jax.sharding import PartitionSpec as P

MESH = pl.DeviceIdType.MESH
Y, Z, X = 2, 8, 4
H, K = 4, 2
ROWS, COLS = Y * Z * X, H * K
PIECE, WIDTH = 32, 512
POINTS = COLS * PIECE
BAND = X * PIECE
HOPS = (0, 1, 7, 2, 6, 3, 5, 4)
BF, F32 = jnp.bfloat16, jnp.float32


def kernel(
    orb_ref, kernel_ref, basis_ref, out_ref,
    col, rows, kern, basis, basis2, acc, packed, packed16, part, proj, proj16, xpart, zsum, zpart, ysum, ypart, fin,
    load_sem, zs, zr, xs, xr, ys, yr, ys2, yr2, xs2, xr2, hs, hr, ks, kr, cs, cr, rxs, rxr, rzs, rzr, rys, ryr, fs, fr,
):
    row, me = lax.axis_index("row"), lax.axis_index("col")
    yl, z, x = row // (Z * X), (row // X) % Z, row % X
    h, k = me // K, me % K

    def at_row(a, b, c):
        return (a * Z + b) * X + c

    def z_dev(d):
        return {"row": at_row(yl, (z + d) % Z, x)}

    def x_dev(e):
        return {"row": at_row(yl, z, (x + e) % X)}

    y_dev = {"row": at_row(1 - yl, z, x)}

    def c_at(dh, dk):
        return ((h + dh) % H) * K + (k + dk) % K

    def c_dev(dh, dk):
        return {"col": c_at(dh, dk)}

    PEERS = [(dh, dk) for dh in (2, 1, 3, 0) for dk in (0, 1) if (dh, dk) != (0, 0)]

    barrier = pltpu.get_barrier_semaphore()
    peers = [z_dev(d) for d in range(1, Z)] + [x_dev(e) for e in range(1, X)] + [y_dev] + [c_dev(*p) for p in PEERS]
    for p in peers:
        pl.semaphore_signal(barrier, inc=1, device_id=p, device_id_type=MESH)

    load_k = pltpu.make_async_copy(kernel_ref, kern, load_sem.at[0])
    load_b = pltpu.make_async_copy(basis_ref, basis, load_sem.at[1])
    load_k.start()
    load_b.start()
    mine = orb_ref[...]
    col[row] = mine
    rows[me] = mine
    pl.semaphore_wait(barrier, len(peers))

    sends = []

    def send(src, dst, s, r, dev):
        c = pltpu.make_async_remote_copy(src, dst, s, r, device_id=dev, device_id_type=MESH)
        c.start()
        sends.append(c)

    def arrived(dst, s, r, dev):
        pltpu.make_async_remote_copy(dst, dst, s, r, device_id=dev, device_id_type=MESH).wait_recv()

    TOP, BOT = pl.ds(0, PIECE // 2), pl.ds(PIECE // 2, PIECE // 2)

    for d in HOPS[1:]:
        send(col.at[row], col.at[row], zs.at[d], zr.at[d], z_dev(d))
    for dh in (2, 1, 3):
        send(rows.at[me], rows.at[me], hs.at[dh], hr.at[dh], c_dev(dh, 0))
    send(rows.at[me], rows.at[me], ks.at[0], kr.at[0], c_dev(0, 1))

    def spread(d):
        i = at_row(yl, (z - d + Z) % Z, x)
        b = col.at[i]
        for e in (2, 1, 3):
            send(b, b, xs.at[d, e], xr.at[d, e], x_dev(e))
        send(b, b, ys.at[d], yr.at[d], y_dev)

    def stage1(d):
        if d:
            i = at_row(yl, (z - d + Z) % Z, x)
            arrived(col.at[i], zs.at[d], zr.at[d], z_dev(d))
        spread(d)

    def stage2(d):
        zb = (z - d + Z) % Z
        for e in (1, 3, 2):
            b = col.at[at_row(yl, zb, (x - e + X) % X)]
            arrived(b, xs.at[d, e], xr.at[d, e], x_dev(e))
            send(b.at[TOP], b.at[TOP], ys2.at[d, e], yr2.at[d, e], y_dev)
        b = col.at[at_row(1 - yl, zb, x)]
        arrived(b, ys.at[d], yr.at[d], y_dev)
        for e in (2, 1, 3):
            send(b.at[BOT], b.at[BOT], xs2.at[d, e], xr2.at[d, e], x_dev(e))

    def stage3(d):
        zb = (z - d + Z) % Z
        for e in (1, 3, 2):
            b = col.at[at_row(1 - yl, zb, (x - e + X) % X)]
            arrived(b.at[TOP], ys2.at[d, e], yr2.at[d, e], y_dev)
            arrived(b.at[BOT], xs2.at[d, e], xr2.at[d, e], x_dev(e))

    def compute(y_at, d, first=False):
        band = y_at * Z + (z - d + Z) % Z
        c = col[pl.ds(band * X, X)].reshape(BAND, WIDTH)
        kk = kern[:, pl.ds(pl.multiple_of(band * BAND, BAND), BAND)].astype(F32)
        for s in range(2):
            sl = slice(s * 256, s * 256 + 256)
            r = rows[:, :, sl].reshape(POINTS, 256)
            den = lax.dot_general(r, c[:, sl], (((1,), (1,)), ((), ())), preferred_element_type=F32)
            w = (den * kk).astype(BF)
            t = jnp.dot(w, c[:, sl], preferred_element_type=F32)
            if first:
                acc[:, sl] = t
            else:
                acc[:, sl] += t

    stage1(HOPS[0])
    load_b.wait()
    for y_at in range(Y):
        basis2[:, y_at * POINTS:(y_at + 1) * POINTS] = basis[:, y_at * 1024:(y_at + 1) * 1024].T
    for dh in (1, 3, 2):
        b = rows.at[c_at(H - dh, 0)]
        arrived(b, hs.at[dh], hr.at[dh], c_dev(dh, 0))
        send(b, b, ks.at[dh], kr.at[dh], c_dev(0, 1))
    stage1(HOPS[1])
    stage1(HOPS[2])
    stage2(HOPS[0])
    for dh in range(H):
        arrived(rows.at[c_at(H - dh, 1)], ks.at[dh], kr.at[dh], c_dev(0, 1))
    load_k.wait()
    for n in range(3, Z + 3):
        if n < Z:
            stage1(HOPS[n])
        if 1 <= n - 2 < Z:
            stage2(HOPS[n - 2])
        if n - 3 < Z:
            compute(yl, HOPS[n - 3], n == 3)
            stage3(HOPS[n - 3])
            compute(1 - yl, HOPS[n - 3])

    low = lax.broadcasted_iota(jnp.int32, (128, 128), 1) < 64
    for q in range(H):
        top, bot = acc[0:128, q * 128:q * 128 + 128], acc[128:256, q * 128:q * 128 + 128]
        for j, v in enumerate((jnp.where(low, top, pltpu.roll(bot, 64, 1)), jnp.where(low, pltpu.roll(top, 64, 1), bot))):
            packed[2 * q + j] = v
            packed16[2 * q + j] = v.astype(BF)
    for dh, dk in PEERS:
        n = dh * K + dk
        send(packed16.at[c_at(dh, dk)], part.at[n], cs.at[n], cr.at[n], c_dev(dh, dk))
    total = packed[me]
    for dh, dk in reversed(PEERS):
        n = dh * K + dk
        arrived(part.at[n], cs.at[n], cr.at[n], c_dev(dh, dk))
        total += part[n].astype(F32)

    t, tr = total.astype(BF).astype(F32), pltpu.roll(total.astype(BF).astype(F32), 64, 1)
    zero = jnp.zeros_like(t)
    rhs = jnp.concatenate([jnp.where(low, t, zero), jnp.where(low, tr, zero), jnp.where(low, zero, tr), jnp.where(low, zero, t)], axis=0).astype(BF)
    e = jnp.dot(basis2[...], rhs, preferred_element_type=F32).reshape(Z, X, PIECE, 128)
    proj[...] = e
    proj16[...] = e.astype(BF)

    for n in (2, 1, 3):
        send(proj16.at[:, (x + n) % X], xpart.at[n], rxs.at[n], rxr.at[n], x_dev(n))
    sums = proj[:, x]
    for n in (1, 3, 2):
        arrived(xpart.at[n], rxs.at[n], rxr.at[n], x_dev(n))
        sums += xpart[n].astype(F32)
    zsum[...] = sums
    for d in (4, 3, 5, 2, 6, 1, 7):
        send(zsum.at[(z + d) % Z], zpart.at[d], rzs.at[d], rzr.at[d], z_dev(d))
    sums = zsum[z]
    for d in HOPS[1:]:
        arrived(zpart.at[d], rzs.at[d], rzr.at[d], z_dev(d))
        sums += zpart[d]
    ysum[...] = sums
    send(ysum, ypart, rys.at[0], ryr.at[0], y_dev)
    arrived(ypart, rys.at[0], ryr.at[0], y_dev)
    sums += ypart[...]

    v = jnp.where(yl == 0, sums, pltpu.roll(sums, 64, 1))
    low = low[0:16]
    fin[me] = jnp.where(low, v[0:16], pltpu.roll(v[16:32], 64, 1))
    for dh, dk in PEERS:
        n = dh * K + dk
        send(fin.at[me], fin.at[me], fs.at[n], fr.at[n], c_dev(dh, dk))
    for dh, dk in reversed(PEERS):
        n = dh * K + dk
        arrived(fin.at[c_at(H - dh, dk)], fs.at[n], fr.at[n], c_dev(dh, dk))
    for q in range(H):
        a, b = fin[2 * q], fin[2 * q + 1]
        out_ref[0:16, q * 128:q * 128 + 128] = jnp.where(low, a, pltpu.roll(b, 64, 1))
        out_ref[16:32, q * 128:q * 128 + 128] = jnp.where(low, pltpu.roll(a, 64, 1), b)
    for c in sends:
        c.wait_send()


def body(orbitals, kern, basis):
    V, D = pltpu.VMEM, pltpu.SemaphoreType.DMA
    out = pl.pallas_call(
        kernel,
        out_shape=jax.ShapeDtypeStruct((PIECE, WIDTH), F32),
        in_specs=[pl.BlockSpec(memory_space=pltpu.VMEM), pl.BlockSpec(memory_space=pl.ANY), pl.BlockSpec(memory_space=pl.ANY)],
        out_specs=pl.BlockSpec(memory_space=pltpu.VMEM),
        scratch_shapes=[
            V((ROWS, PIECE, WIDTH), BF), V((COLS, PIECE, WIDTH), BF), V((POINTS, 2048), BF), V((POINTS, 2048), BF),
            V((1024, 512), BF), V((POINTS, WIDTH), F32), V((COLS, 128, 128), F32), V((COLS, 128, 128), BF),
            V((COLS, 128, 128), BF), V((Z, X, PIECE, 128), F32), V((Z, X, PIECE, 128), BF), V((X, Z, PIECE, 128), BF),
            V((Z, PIECE, 128), F32), V((Z, PIECE, 128), F32), V((PIECE, 128), F32), V((PIECE, 128), F32), V((COLS, 16, 128), F32),
            D((2,)),
            D((Z,)), D((Z,)), D((Z, X)), D((Z, X)), D((Z,)), D((Z,)), D((Z, X)), D((Z, X)), D((Z, X)), D((Z, X)),
            D((H,)), D((H,)), D((H,)), D((H,)), D((COLS,)), D((COLS,)), D((X,)), D((X,)), D((Z,)), D((Z,)), D((1,)), D((1,)),
            D((COLS,)), D((COLS,)),
        ],
        compiler_params=pltpu.CompilerParams(collective_id=0, has_side_effects=True, vmem_limit_bytes=48 << 20),
        cost_estimate=pl.CostEstimate(flops=1_300_000_000, bytes_accessed=2_300_000, transcendentals=0),
        name="exchange",
    )(orbitals.reshape(PIECE, WIDTH), kern, basis)
    return out.reshape(PIECE, 2, WIDTH // 2)


def solution(mesh):
    return jax.shard_map(
        body,
        mesh=mesh,
        in_specs=(P(("row", "col"), None, None), P("row", "col"), P("row", None)),
        out_specs=P("row", None, None),
        check_vma=False,
    )
```

```python
import jax
import jax.numpy as jnp
from jax import lax
from jax.experimental import pallas as pl
from jax.experimental.pallas import tpu as pltpu
from jax.sharding import PartitionSpec as P

MESH = pl.DeviceIdType.MESH
Y, Z, X = 2, 8, 4
H, K = 4, 2
ROWS, COLS = Y * Z * X, H * K
PIECE, WIDTH = 32, 512
POINTS = COLS * PIECE
BAND = X * PIECE
HOPS = (0, 1, 7, 2, 6, 3, 5, 4)
FAR = 4
SCHEDULE = (
    "s0", "t0", "B", "s1", "s7", "c0", "s2", "s6", "c1", "s3", "s5", "R",
    "c7", "s4", "Z", "r0", "c2", "c6", "r1", "r7", "I", "c3", "n0", "c5",
    "r2", "f0", "r6", "n1", "c4", "t1", "t7", "n7", "t4", "t2", "r3", "n2",
    "t6", "r5", "n6", "t3", "t5", "f1", "r4", "f7", "n3", "n5", "f2", "n4",
    "f6", "f3", "f5", "f4",
)
BF, F32 = jnp.bfloat16, jnp.float32


def kernel(
    orb_ref, kernel_ref, basis_ref, out_ref,
    orb, col, rows, kern, basis, basis2, acc, packed, pairs, send16, part, proj, proj16, xpart, zsum, zpart, fin,
    load_sem, sent, zr, zr2, xr, xr3, yr, lr, hr, kr, pr, cr, rxr, rzr, fr,
):
    row, me = lax.axis_index("row"), lax.axis_index("col")
    yl, z, x = row // (Z * X), (row // X) % Z, row % X
    h, k = me // K, me % K

    def at_row(a, b, c):
        return (a * Z + b) * X + c

    def z_dev(d):
        return {"row": at_row(yl, (z + d) % Z, x)}

    def x_dev(e):
        return {"row": at_row(yl, z, (x + e) % X)}

    y_dev = {"row": at_row(1 - yl, z, x)}

    def xy_dev(n):
        return {"row": at_row((yl + n // X) % Y, z, (x + n % X) % X)}

    def c_at(dh, dk):
        return ((h + dh) % H) * K + (k + dk) % K

    def c_dev(dh, dk):
        return {"col": c_at(dh, dk)}

    PEERS = [(dh, dk) for dh in (2, 1, 3, 0) for dk in (0, 1) if (dh, dk) != (0, 0)]

    barrier = pltpu.get_barrier_semaphore()
    peers = [z_dev(d) for d in range(1, Z)] + [xy_dev(n) for n in range(1, X * Y)] + [c_dev(*p) for p in PEERS]
    for p in peers:
        pl.semaphore_signal(barrier, inc=1, device_id=p, device_id_type=MESH)

    load_o = pltpu.make_async_copy(orb_ref, orb, load_sem.at[0])
    load_k = pltpu.make_async_copy(kernel_ref, kern, load_sem.at[1])
    load_b = pltpu.make_async_copy(basis_ref, basis, load_sem.at[2])
    load_o.start()
    load_k.start()
    load_b.start()
    load_o.wait()
    for s in range(2):
        mine = orb[:, s, :]
        col[row, :, s * 256:s * 256 + 256] = mine
        rows[me, :, s * 256:s * 256 + 256] = mine
    pl.semaphore_wait(barrier, len(peers))

    def send(src, dst, group, arrival, dev):
        pltpu.make_async_remote_copy(src, dst, sent.at[group], arrival, device_id=dev, device_id_type=MESH).start()

    def arrived(like, arrival):
        pltpu.make_async_copy(like, like, arrival).wait()

    HALVES = pl.ds(0, 256), pl.ds(256, 256)

    def block(y_at, d, e=0):
        return col.at[at_row(y_at, (z - d + Z) % Z, (x - e + X) % X)]

    own = col.at[row]
    send(own, own, 0, yr.at[0], y_dev)
    for d in HOPS[1:]:
        send(own, own, 0, zr.at[d], z_dev(d))
    for dh in (2, 1, 3):
        send(rows.at[me], rows.at[me], 1, hr.at[dh], c_dev(dh, 0))
    send(rows.at[me], rows.at[me], 1, kr.at[0], c_dev(0, 1))

    def spread(d):
        b = block(yl, d)
        if d:
            arrived(b, zr.at[d])
        for e in (1, 3):
            send(b, b, 2, xr.at[d], x_dev(e))
        if d == FAR:
            send(b, b, 0, yr.at[1], y_dev)

    def cross(d):
        arrived(col.at[pl.ds(0, 2)], xr.at[d])
        for n, e in enumerate((1, 3)):
            half = block(yl, d, e).at[:, HALVES[n]]
            send(half, half, 3, xr3.at[d], x_dev(e))
        for e in (1, 3):
            half = block(yl, d, e).at[:, HALVES[0]]
            send(half, half, 4, lr.at[d], y_dev)

    def relay(d):
        b = block(yl, d, 2)
        arrived(b, xr3.at[d])
        send(b, b, 5, lr.at[d], y_dev)

    def fan():
        b = block(1 - yl, 0)
        for d in HOPS[1:-1]:
            send(b, b, 1, zr2.at[d], z_dev(d))

    def spread2(d):
        b = block(1 - yl, d)
        arrived(b, yr.at[d // FAR] if d in (0, FAR) else zr2.at[d])
        half = b.at[:, HALVES[1]]
        for e in (1, 3):
            send(half, half, 6, lr.at[d], x_dev(e))

    def last(d):
        arrived(col.at[pl.ds(0, 3)], lr.at[d])

    def rows_on():
        for dh in (1, 3, 2):
            b = rows.at[c_at(H - dh, 0)]
            arrived(b, hr.at[dh])
            send(b, b, 1, kr.at[0], c_dev(0, 1))

    def rows_in():
        arrived(rows.at[pl.ds(0, 4)], kr.at[0])
        load_k.wait()

    def prepare():
        load_b.wait()
        for half in range(2):
            t = basis[:, half * 1024:half * 1024 + 1024].T.reshape(ROWS // 2, 2, PIECE // 2, POINTS)
            for q in range(2):
                basis2[half * 512:half * 512 + 512, q * POINTS:q * POINTS + POINTS] = t[:, q].reshape(512, POINTS)

    def compute(y_at, d, first=False):
        band = y_at * Z + (z - d + Z) % Z
        c = col[pl.ds(band * X, X)].reshape(BAND, WIDTH)
        kk = kern[:, pl.ds(pl.multiple_of(band * BAND, BAND), BAND)].astype(F32)
        for s in range(2):
            sl = slice(s * 256, s * 256 + 256)
            r = rows[:, :, sl].reshape(POINTS, 256)
            den = lax.dot_general(r, c[:, sl], (((1,), (1,)), ((), ())), preferred_element_type=F32)
            w = (den * kk).astype(BF)
            t = jnp.dot(w, c[:, sl], preferred_element_type=F32)
            if first:
                acc[:, sl] = t
            else:
                acc[:, sl] += t

    started = []

    def near(d):
        compute(yl, d, not started)
        started.append(d)

    def far(d):
        last(d)
        compute(1 - yl, d)

    steps = {"s": spread, "c": cross, "r": relay, "t": spread2, "n": near, "f": far, "Z": lambda _: fan(), "R": lambda _: rows_on(), "I": lambda _: rows_in(), "B": lambda _: prepare()}
    for step in SCHEDULE:
        steps[step[0]](int(step[1:] or 0))

    low = lax.broadcasted_iota(jnp.int32, (128, 128), 1) < 64
    for q in range(H):
        top, bot = acc[0:128, q * 128:q * 128 + 128], acc[128:256, q * 128:q * 128 + 128]
        packed[q, 0] = jnp.where(low, top, pltpu.roll(bot, 64, 1))
        packed[q, 1] = jnp.where(low, pltpu.roll(top, 64, 1), bot)
    for dh in (2, 1, 3, 0):
        send(packed.at[(h + dh) % H, 1 - k], pairs.at[dh], 7, pr.at[dh], c_dev(0, 1))
    for dh in (2, 1, 3):
        arrived(pairs.at[dh], pr.at[dh])
        send16[dh] = (packed[(h + dh) % H, k] + pairs[dh]).astype(BF)
        send(send16.at[dh], part.at[dh - 1], 8, cr.at[0], c_dev(dh, 0))
    arrived(pairs.at[0], pr.at[0])
    total = packed[h, k] + pairs[0]
    arrived(part, cr.at[0])
    for n in range(H - 1):
        total += part[n].astype(F32)

    t, tr = total.astype(BF).astype(F32), pltpu.roll(total.astype(BF).astype(F32), 64, 1)
    zero = jnp.zeros_like(t)
    rhs = jnp.concatenate([jnp.where(low, t, zero), jnp.where(low, tr, zero), jnp.where(low, zero, tr), jnp.where(low, zero, t)], axis=0).astype(BF)
    e = jnp.dot(basis2[...], rhs, preferred_element_type=F32).reshape(Y, Z, X, PIECE // 2, 128)
    proj[...] = e
    proj16[...] = e.astype(BF)

    for n in (6, 5, 7, 2, 4, 1, 3):
        send(proj16.at[(yl + n // X) % Y, :, (x + n % X) % X], xpart.at[n - 1], 9, rxr.at[0], xy_dev(n))
    sums = proj[yl, :, x]
    arrived(xpart, rxr.at[0])
    for n in range(X * Y - 1):
        sums += xpart[n].astype(F32)
    zsum[...] = sums
    for d in (4, 3, 5, 2, 6, 1, 7):
        send(zsum.at[(z + d) % Z], zpart.at[d - 1], 10, rzr.at[0], z_dev(d))
    sums = zsum[z]
    arrived(zpart, rzr.at[0])
    for n in range(Z - 1):
        sums += zpart[n]

    fin[me] = sums
    low = low[0:16]
    for dh, dk in PEERS:
        send(fin.at[me], fin.at[me], 11, fr.at[0], c_dev(dh, dk))
    arrived(fin.at[pl.ds(0, COLS - 1)], fr.at[0])
    for q in range(H):
        a, b = fin[2 * q], fin[2 * q + 1]
        sl = slice(q % 2 * 128, q % 2 * 128 + 128)
        out_ref[0:16, q // 2, sl] = jnp.where(low, a, pltpu.roll(b, 64, 1))
        out_ref[16:32, q // 2, sl] = jnp.where(low, pltpu.roll(a, 64, 1), b)
    arrived(col.at[pl.ds(0, 9)], sent.at[0])
    arrived(col.at[pl.ds(0, 13)], sent.at[1])
    arrived(col.at[pl.ds(0, 16)], sent.at[2])
    for n in (3, 4, 5, 6):
        arrived(col.at[pl.ds(0, 8)], sent.at[n])
    arrived(pairs, sent.at[7])
    arrived(part, sent.at[8])
    arrived(xpart, sent.at[9])
    arrived(zpart, sent.at[10])
    arrived(fin.at[pl.ds(0, COLS - 1)], sent.at[11])


def body(orbitals, kern, basis):
    V, D = pltpu.VMEM, pltpu.SemaphoreType.DMA
    return pl.pallas_call(
        kernel,
        out_shape=jax.ShapeDtypeStruct((PIECE, 2, WIDTH // 2), F32),
        in_specs=[pl.BlockSpec(memory_space=pltpu.HBM), pl.BlockSpec(memory_space=pltpu.HBM), pl.BlockSpec(memory_space=pltpu.HBM)],
        out_specs=pl.BlockSpec(memory_space=pltpu.VMEM),
        scratch_shapes=[
            V((PIECE, 2, WIDTH // 2), BF), V((ROWS, PIECE, WIDTH), BF), V((COLS, PIECE, WIDTH), BF), V((POINTS, 2048), BF), V((POINTS, 2048), BF),
            V((1024, 512), BF), V((POINTS, WIDTH), F32), V((H, K, 128, 128), F32), V((H, 128, 128), F32), V((H, 128, 128), BF),
            V((H - 1, 128, 128), BF), V((Y, Z, X, 16, 128), F32), V((Y, Z, X, 16, 128), BF), V((X * Y - 1, Z, 16, 128), BF),
            V((Z, 16, 128), F32), V((Z - 1, 16, 128), F32), V((COLS, 16, 128), F32),
            D((3,)), D((12,)), D((Z,)), D((Z,)), D((Z,)), D((Z,)), D((2,)), D((Z,)), D((H,)), D((1,)), D((H,)), D((1,)), D((1,)), D((1,)), D((1,)),
        ],
        compiler_params=pltpu.CompilerParams(collective_id=0, has_side_effects=True, vmem_limit_bytes=61 << 20),
        cost_estimate=pl.CostEstimate(flops=1_300_000_000, bytes_accessed=2_300_000, transcendentals=0),
        name="exchange",
    )(orbitals, kern, basis)


def solution(mesh):
    return jax.shard_map(
        body,
        mesh=mesh,
        in_specs=(P(("row", "col"), None, None), P("row", "col"), P("row", None)),
        out_specs=P("row", None, None),
        check_vma=False,
    )
```

```python
import jax
import jax.numpy as jnp
from jax import lax
from jax.experimental import pallas as pl
from jax.experimental.pallas import tpu as pltpu
from jax.sharding import PartitionSpec as P

MESH = pl.DeviceIdType.MESH
Y, Z, X = 2, 8, 4
H, K = 4, 2
ROWS, COLS = Y * Z * X, H * K
PIECE, WIDTH = 32, 512
POINTS = COLS * PIECE
BAND = X * PIECE
HOPS = (0, 1, 7, 2, 6, 3, 5, 4)
FAR = 4
SCHEDULE = (
    "s0", "t0", "B", "s1", "s7", "c0", "s2", "s6", "c1", "s3", "s5", "R",
    "c7", "s4", "Z", "r0", "c2", "c6", "r1", "r7", "I", "c3", "n0", "c5",
    "r2", "f0", "r6", "n1", "c4", "t1", "t7", "n7", "t4", "t2", "r3", "n2",
    "t6", "r5", "n6", "t3", "t5", "f1", "r4", "f7", "n3", "n5", "f2", "n4",
    "f6", "f3", "f5", "f4",
)
BF, F32 = jnp.bfloat16, jnp.float32


def kernel(
    orb_ref, kernel_ref, basis_ref, out_ref,
    orb, col, rows, kern, basis, basis2, acc, packed, pairs, send16, part, proj, proj16, xpart, zsum, zpart, fin,
    load_sem, sent, zr, zr2, xr, xr3, yr, lr, hr, kr, pr, cr, rxr, rzr, fr,
):
    row, me = lax.axis_index("row"), lax.axis_index("col")
    yl, z, x = row // (Z * X), (row // X) % Z, row % X
    h, k = me // K, me % K

    def at_row(a, b, c):
        return (a * Z + b) * X + c

    def z_dev(d):
        return {"row": at_row(yl, (z + d) % Z, x)}

    def x_dev(e):
        return {"row": at_row(yl, z, (x + e) % X)}

    y_dev = {"row": at_row(1 - yl, z, x)}

    def xy_dev(n):
        return {"row": at_row((yl + n // X) % Y, z, (x + n % X) % X)}

    def c_at(dh, dk):
        return ((h + dh) % H) * K + (k + dk) % K

    def c_dev(dh, dk):
        return {"col": c_at(dh, dk)}

    PEERS = [(dh, dk) for dh in (2, 1, 3, 0) for dk in (0, 1) if (dh, dk) != (0, 0)]

    barrier = pltpu.get_barrier_semaphore()
    peers = [z_dev(d) for d in range(1, Z)] + [xy_dev(n) for n in range(1, X * Y)] + [c_dev(*p) for p in PEERS]
    for p in peers:
        pl.semaphore_signal(barrier, inc=1, device_id=p, device_id_type=MESH)

    load_o = pltpu.make_async_copy(orb_ref, orb, load_sem.at[0])
    load_k = pltpu.make_async_copy(kernel_ref, kern, load_sem.at[1])
    load_b = pltpu.make_async_copy(basis_ref, basis, load_sem.at[2])
    load_o.start()
    load_k.start()
    load_b.start()
    load_o.wait()
    for s in range(2):
        mine = orb[:, s, :]
        col[row, :, s * 256:s * 256 + 256] = mine
        rows[me, :, s * 256:s * 256 + 256] = mine
    pl.semaphore_wait(barrier, len(peers))

    def send(src, dst, group, arrival, dev):
        pltpu.make_async_remote_copy(src, dst, sent.at[group], arrival, device_id=dev, device_id_type=MESH).start()

    def arrived(like, arrival):
        pltpu.make_async_copy(like, like, arrival).wait()

    HALVES = pl.ds(0, 256), pl.ds(256, 256)

    def block(y_at, d, e=0):
        return col.at[at_row(y_at, (z - d + Z) % Z, (x - e + X) % X)]

    own = col.at[row]
    send(own, own, 0, yr.at[0], y_dev)
    for d in HOPS[1:]:
        send(own, own, 0, zr.at[d], z_dev(d))
    for dh in (2, 1, 3):
        send(rows.at[me], rows.at[me], 1, hr.at[dh], c_dev(dh, 0))
    send(rows.at[me], rows.at[me], 1, kr.at[0], c_dev(0, 1))

    def spread(d):
        b = block(yl, d)
        if d:
            arrived(b, zr.at[d])
        for e in (1, 3):
            send(b, b, 2, xr.at[d], x_dev(e))
        if d == FAR:
            send(b, b, 0, yr.at[1], y_dev)

    def cross(d):
        arrived(col.at[pl.ds(0, 2)], xr.at[d])
        for n, e in enumerate((1, 3)):
            half = block(yl, d, e).at[:, HALVES[n]]
            send(half, half, 3, xr3.at[d], x_dev(e))
        for e in (1, 3):
            half = block(yl, d, e).at[:, HALVES[0]]
            send(half, half, 4, lr.at[d], y_dev)

    def relay(d):
        b = block(yl, d, 2)
        arrived(b, xr3.at[d])
        send(b, b, 5, lr.at[d], y_dev)

    def fan():
        b = block(1 - yl, 0)
        for d in HOPS[1:-1]:
            send(b, b, 1, zr2.at[d], z_dev(d))

    def spread2(d):
        b = block(1 - yl, d)
        arrived(b, yr.at[d // FAR] if d in (0, FAR) else zr2.at[d])
        half = b.at[:, HALVES[1]]
        for e in (1, 3):
            send(half, half, 6, lr.at[d], x_dev(e))

    def last(d):
        arrived(col.at[pl.ds(0, 3)], lr.at[d])

    def rows_on():
        for dh in (1, 3, 2):
            b = rows.at[c_at(H - dh, 0)]
            arrived(b, hr.at[dh])
            send(b, b, 1, kr.at[0], c_dev(0, 1))

    def rows_in():
        arrived(rows.at[pl.ds(0, 4)], kr.at[0])
        load_k.wait()

    def prepare():
        load_b.wait()
        for half in range(2):
            t = basis[:, half * 1024:half * 1024 + 1024].T.reshape(ROWS // 2, 2, PIECE // 2, POINTS)
            for q in range(2):
                basis2[half * 512:half * 512 + 512, q * POINTS:q * POINTS + POINTS] = t[:, q].reshape(512, POINTS)

    def compute(y_at, d, first=False):
        band = y_at * Z + (z - d + Z) % Z
        c = col[pl.ds(band * X, X)].reshape(BAND, WIDTH)
        kk = kern[:, pl.ds(pl.multiple_of(band * BAND, BAND), BAND)].astype(F32)
        for s in range(2):
            sl = slice(s * 256, s * 256 + 256)
            r = rows[:, :, sl].reshape(POINTS, 256)
            den = lax.dot_general(r, c[:, sl], (((1,), (1,)), ((), ())), preferred_element_type=F32)
            w = (den * kk).astype(BF)
            t = jnp.dot(w, c[:, sl], preferred_element_type=F32)
            if first:
                acc[:, sl] = t
            else:
                acc[:, sl] += t

    started = []

    def near(d):
        compute(yl, d, not started)
        started.append(d)

    def far(d):
        last(d)
        compute(1 - yl, d)

    steps = {"s": spread, "c": cross, "r": relay, "t": spread2, "n": near, "f": far, "Z": lambda _: fan(), "R": lambda _: rows_on(), "I": lambda _: rows_in(), "B": lambda _: prepare()}
    for step in SCHEDULE:
        steps[step[0]](int(step[1:] or 0))

    low = lax.broadcasted_iota(jnp.int32, (128, 128), 1) < 64
    for q in range(H):
        top, bot = acc[0:128, q * 128:q * 128 + 128], acc[128:256, q * 128:q * 128 + 128]
        packed[q, 0] = jnp.where(low, top, pltpu.roll(bot, 64, 1))
        packed[q, 1] = jnp.where(low, pltpu.roll(top, 64, 1), bot)
    for dh in (2, 1, 3, 0):
        send(packed.at[(h + dh) % H, 1 - k], pairs.at[dh], 7, pr.at[dh], c_dev(0, 1))
    for dh in (2, 1, 3):
        arrived(pairs.at[dh], pr.at[dh])
        send16[dh] = (packed[(h + dh) % H, k] + pairs[dh]).astype(BF)
        send(send16.at[dh], part.at[dh - 1], 8, cr.at[0], c_dev(dh, 0))
    arrived(pairs.at[0], pr.at[0])
    total = packed[h, k] + pairs[0]
    arrived(part, cr.at[0])
    for n in range(H - 1):
        total += part[n].astype(F32)

    t, tr = total.astype(BF).astype(F32), pltpu.roll(total.astype(BF).astype(F32), 64, 1)
    zero = jnp.zeros_like(t)
    rhs = jnp.concatenate([jnp.where(low, t, zero), jnp.where(low, tr, zero), jnp.where(low, zero, tr), jnp.where(low, zero, t)], axis=0).astype(BF)
    HALF = Z // 2
    for half in range(2):
        zz = slice(half * HALF, half * HALF + HALF)
        for y_at in range(Y):
            r0 = (y_at * Z + half * HALF) * X * 16
            e = jnp.dot(basis2[r0:r0 + HALF * X * 16], rhs, preferred_element_type=F32).reshape(HALF, X, 16, 128)
            proj[y_at, zz] = e
            proj16[y_at, zz] = e.astype(BF)
        for n in (6, 5, 7, 2, 4, 1, 3):
            piece = proj16.at[(yl + n // X) % Y, pl.ds(half * HALF, HALF), (x + n % X) % X]
            send(piece, xpart.at[half, n - 1], 9, rxr.at[half], xy_dev(n))
    for half in range(2):
        zz = slice(half * HALF, half * HALF + HALF)
        sums = proj[yl, zz, x]
        arrived(xpart.at[half], rxr.at[half])
        for n in range(X * Y - 1):
            sums += xpart[half, n].astype(F32)
        zsum[zz] = sums
        for t in range(half * HALF, half * HALF + HALF):

            @pl.when(z != t)
            def _(t=t):
                send(zsum.at[t], zpart.at[z], 10, rzr.at[0], {"row": at_row(yl, t, x)})

    zpart[z] = zsum[z]
    arrived(zpart.at[pl.ds(0, Z - 1)], rzr.at[0])
    sums = zpart[0]
    for n in range(1, Z):
        sums += zpart[n]

    fin[me] = sums
    low = low[0:16]
    for dh, dk in PEERS:
        send(fin.at[me], fin.at[me], 11, fr.at[0], c_dev(dh, dk))
    arrived(fin.at[pl.ds(0, COLS - 1)], fr.at[0])
    for q in range(H):
        a, b = fin[2 * q], fin[2 * q + 1]
        sl = slice(q % 2 * 128, q % 2 * 128 + 128)
        out_ref[0:16, q // 2, sl] = jnp.where(low, a, pltpu.roll(b, 64, 1))
        out_ref[16:32, q // 2, sl] = jnp.where(low, pltpu.roll(a, 64, 1), b)
    arrived(col.at[pl.ds(0, 9)], sent.at[0])
    arrived(col.at[pl.ds(0, 13)], sent.at[1])
    arrived(col.at[pl.ds(0, 16)], sent.at[2])
    for n in (3, 4, 5, 6):
        arrived(col.at[pl.ds(0, 8)], sent.at[n])
    arrived(pairs, sent.at[7])
    arrived(part, sent.at[8])
    arrived(xpart, sent.at[9])
    arrived(zpart.at[pl.ds(0, Z - 1)], sent.at[10])
    arrived(fin.at[pl.ds(0, COLS - 1)], sent.at[11])


def body(orbitals, kern, basis):
    V, D = pltpu.VMEM, pltpu.SemaphoreType.DMA
    return pl.pallas_call(
        kernel,
        out_shape=jax.ShapeDtypeStruct((PIECE, 2, WIDTH // 2), F32),
        in_specs=[pl.BlockSpec(memory_space=pltpu.HBM), pl.BlockSpec(memory_space=pltpu.HBM), pl.BlockSpec(memory_space=pltpu.HBM)],
        out_specs=pl.BlockSpec(memory_space=pltpu.VMEM),
        scratch_shapes=[
            V((PIECE, 2, WIDTH // 2), BF), V((ROWS, PIECE, WIDTH), BF), V((COLS, PIECE, WIDTH), BF), V((POINTS, 2048), BF), V((POINTS, 2048), BF),
            V((1024, 512), BF), V((POINTS, WIDTH), F32), V((H, K, 128, 128), F32), V((H, 128, 128), F32), V((H, 128, 128), BF),
            V((H - 1, 128, 128), BF), V((Y, Z, X, 16, 128), F32), V((Y, Z, X, 16, 128), BF), V((2, X * Y - 1, Z // 2, 16, 128), BF),
            V((Z, 16, 128), F32), V((Z, 16, 128), F32), V((COLS, 16, 128), F32),
            D((3,)), D((12,)), D((Z,)), D((Z,)), D((Z,)), D((Z,)), D((2,)), D((Z,)), D((H,)), D((1,)), D((H,)), D((1,)), D((2,)), D((1,)), D((1,)),
        ],
        compiler_params=pltpu.CompilerParams(collective_id=0, has_side_effects=True, vmem_limit_bytes=53 << 20),
        cost_estimate=pl.CostEstimate(flops=1_300_000_000, bytes_accessed=2_300_000, transcendentals=0),
        name="exchange",
    )(orbitals, kern, basis)


def solution(mesh):
    return jax.shard_map(
        body,
        mesh=mesh,
        in_specs=(P(("row", "col"), None, None), P("row", "col"), P("row", None)),
        out_specs=P("row", None, None),
        check_vma=False,
    )
```

```python
import functools

import jax
import jax.numpy as jnp
from jax import lax
from jax.experimental import pallas as pl
from jax.experimental.pallas import tpu as pltpu
from jax.sharding import PartitionSpec as P

MESH = pl.DeviceIdType.MESH
Y, Z, X = 2, 8, 4
H, K = 4, 2
ROWS, COLS = Y * Z * X, H * K
PIECE, WIDTH = 32, 512
POINTS = COLS * PIECE
BAND = X * PIECE
HOPS = (0, 1, 7, 2, 6, 3, 5, 4)
FAR = 4
SCHEDULE = (
    "s0", "t0", "B", "s1", "s7", "c0", "s2", "s6", "c1", "s3", "s5", "R",
    "c7", "s4", "Z", "r0", "c2", "c6", "r1", "r7", "I", "c3", "n0", "c5",
    "r2", "f0", "r6", "n1", "c4", "t1", "t7", "n7", "t4", "t2", "r3", "n2",
    "t6", "r5", "n6", "t3", "t5", "f1", "r4", "f7", "n3", "n5", "f2", "n4",
    "f6", "f3", "f5", "f4",
)
BF, F32 = jnp.bfloat16, jnp.float32


def kernel(
    orb_ref, kernel_ref, basis_ref, out_ref,
    orb, col, rows, kern, basis, basis2, acc, packed, pairs, send16, part, proj, proj16, xpart, zsum, zpart, fin,
    load_sem, sent, zr, zr2, xr, xr3, yr, lr, hr, kr, pr, cr, rxr, rzr, fr,
):
    row, me = lax.axis_index("row"), lax.axis_index("col")
    yl, z, x = row // (Z * X), (row // X) % Z, row % X
    h, k = me // K, me % K

    def at_row(a, b, c):
        return (a * Z + b) * X + c

    @functools.cache
    def z_dev(d):
        return {"row": at_row(yl, (z + d) % Z, x)}

    @functools.cache
    def x_dev(e):
        return {"row": at_row(yl, z, (x + e) % X)}

    y_dev = {"row": at_row(1 - yl, z, x)}

    @functools.cache
    def xy_dev(n):
        return {"row": at_row((yl + n // X) % Y, z, (x + n % X) % X)}

    @functools.cache
    def c_at(dh, dk):
        return ((h + dh) % H) * K + (k + dk) % K

    @functools.cache
    def c_dev(dh, dk):
        return {"col": c_at(dh, dk)}

    PEERS = [(dh, dk) for dh in (2, 1, 3, 0) for dk in (0, 1) if (dh, dk) != (0, 0)]

    barrier = pltpu.get_barrier_semaphore()
    peers = [z_dev(d) for d in range(1, Z)] + [xy_dev(n) for n in range(1, X * Y)] + [c_dev(*p) for p in PEERS]
    for p in peers:
        pl.semaphore_signal(barrier, inc=1, device_id=p, device_id_type=MESH)

    load_o = pltpu.make_async_copy(orb_ref, orb, load_sem.at[0])
    load_k = pltpu.make_async_copy(kernel_ref, kern, load_sem.at[1])
    load_b = pltpu.make_async_copy(basis_ref, basis, load_sem.at[2])
    load_o.start()
    load_k.start()
    load_b.start()
    load_o.wait()
    for s in range(2):
        mine = orb[:, s, :]
        col[row, :, s * 256:s * 256 + 256] = mine
        rows[me, :, s * 256:s * 256 + 256] = mine
    pl.semaphore_wait(barrier, len(peers))

    def send(src, dst, group, arrival, dev):
        pltpu.make_async_remote_copy(src, dst, sent.at[group], arrival, device_id=dev, device_id_type=MESH).start()

    def arrived(like, arrival):
        pltpu.make_async_copy(like, like, arrival).wait()

    HALVES = pl.ds(0, 256), pl.ds(256, 256)

    places = {}

    def block(y_at, d, e=0):
        other = y_at is not yl
        if (other, d, e) not in places:
            places[other, d, e] = at_row(1 - yl if other else yl, (z - d + Z) % Z, (x - e + X) % X)
        return col.at[places[other, d, e]]

    own = col.at[row]
    send(own, own, 0, yr.at[0], y_dev)
    for d in HOPS[1:]:
        send(own, own, 0, zr.at[d], z_dev(d))
    for dh in (2, 1, 3):
        send(rows.at[me], rows.at[me], 1, hr.at[dh], c_dev(dh, 0))
    send(rows.at[me], rows.at[me], 1, kr.at[0], c_dev(0, 1))

    def spread(d):
        b = block(yl, d)
        if d:
            arrived(b, zr.at[d])
        for e in (1, 3):
            send(b, b, 2, xr.at[d], x_dev(e))
        if d == FAR:
            send(b, b, 0, yr.at[1], y_dev)

    def cross(d):
        arrived(col.at[pl.ds(0, 2)], xr.at[d])
        for n, e in enumerate((1, 3)):
            half = block(yl, d, e).at[:, HALVES[n]]
            send(half, half, 3, xr3.at[d], x_dev(e))
        for e in (1, 3):
            half = block(yl, d, e).at[:, HALVES[0]]
            send(half, half, 4, lr.at[d], y_dev)

    def relay(d):
        b = block(yl, d, 2)
        arrived(b, xr3.at[d])
        send(b, b, 5, lr.at[d], y_dev)

    def fan():
        b = block(1 - yl, 0)
        for d in HOPS[1:-1]:
            send(b, b, 1, zr2.at[d], z_dev(d))

    def spread2(d):
        b = block(1 - yl, d)
        arrived(b, yr.at[d // FAR] if d in (0, FAR) else zr2.at[d])
        half = b.at[:, HALVES[1]]
        for e in (1, 3):
            send(half, half, 6, lr.at[d], x_dev(e))

    def last(d):
        arrived(col.at[pl.ds(0, 3)], lr.at[d])

    def rows_on():
        for dh in (1, 3, 2):
            b = rows.at[c_at(H - dh, 0)]
            arrived(b, hr.at[dh])
            send(b, b, 1, kr.at[0], c_dev(0, 1))

    def rows_in():
        arrived(rows.at[pl.ds(0, 4)], kr.at[0])
        load_k.wait()

    def prepare():
        load_b.wait()
        for half in range(2):
            t = basis[:, half * 1024:half * 1024 + 1024].T.reshape(ROWS // 2, 2, PIECE // 2, POINTS)
            for q in range(2):
                basis2[half * 512:half * 512 + 512, q * POINTS:q * POINTS + POINTS] = t[:, q].reshape(512, POINTS)

    def compute(y_at, d, first=False):
        band = y_at * Z + (z - d + Z) % Z
        c = col[pl.ds(band * X, X)].reshape(BAND, WIDTH)
        kk = kern[:, pl.ds(pl.multiple_of(band * BAND, BAND), BAND)].astype(F32)
        for s in range(2):
            sl = slice(s * 256, s * 256 + 256)
            r = rows[:, :, sl].reshape(POINTS, 256)
            den = lax.dot_general(r, c[:, sl], (((1,), (1,)), ((), ())), preferred_element_type=F32)
            w = (den * kk).astype(BF)
            t = jnp.dot(w, c[:, sl], preferred_element_type=F32)
            if first:
                acc[:, sl] = t
            else:
                acc[:, sl] += t

    started = []

    def near(d):
        compute(yl, d, not started)
        started.append(d)

    def far(d):
        last(d)
        compute(1 - yl, d)

    steps = {"s": spread, "c": cross, "r": relay, "t": spread2, "n": near, "f": far, "Z": lambda _: fan(), "R": lambda _: rows_on(), "I": lambda _: rows_in(), "B": lambda _: prepare()}
    for step in SCHEDULE:
        steps[step[0]](int(step[1:] or 0))

    low = lax.broadcasted_iota(jnp.int32, (128, 128), 1) < 64
    for q in range(H):
        top, bot = acc[0:128, q * 128:q * 128 + 128], acc[128:256, q * 128:q * 128 + 128]
        packed[q, 0] = jnp.where(low, top, pltpu.roll(bot, 64, 1))
        packed[q, 1] = jnp.where(low, pltpu.roll(top, 64, 1), bot)
    for dh in (2, 1, 3, 0):
        send(packed.at[(h + dh) % H, 1 - k], pairs.at[dh], 7, pr.at[dh], c_dev(0, 1))
    for dh in (2, 1, 3):
        arrived(pairs.at[dh], pr.at[dh])
        send16[dh] = (packed[(h + dh) % H, k] + pairs[dh]).astype(BF)
        send(send16.at[dh], part.at[dh - 1], 8, cr.at[0], c_dev(dh, 0))
    arrived(pairs.at[0], pr.at[0])
    total = packed[h, k] + pairs[0]
    arrived(part, cr.at[0])
    for n in range(H - 1):
        total += part[n].astype(F32)

    t, tr = total.astype(BF).astype(F32), pltpu.roll(total.astype(BF).astype(F32), 64, 1)
    zero = jnp.zeros_like(t)
    rhs = jnp.concatenate([jnp.where(low, t, zero), jnp.where(low, tr, zero), jnp.where(low, zero, tr), jnp.where(low, zero, t)], axis=0).astype(BF)
    HALF = Z // 2
    for half in range(2):
        zz = slice(half * HALF, half * HALF + HALF)
        for y_at in range(Y):
            r0 = (y_at * Z + half * HALF) * X * 16
            e = jnp.dot(basis2[r0:r0 + HALF * X * 16], rhs, preferred_element_type=F32).reshape(HALF, X, 16, 128)
            proj[y_at, zz] = e
            proj16[y_at, zz] = e.astype(BF)
        for n in (6, 5, 7, 2, 4, 1, 3):
            piece = proj16.at[(yl + n // X) % Y, pl.ds(half * HALF, HALF), (x + n % X) % X]
            send(piece, xpart.at[half, n - 1], 9, rxr.at[half], xy_dev(n))
    for half in range(2):
        zz = slice(half * HALF, half * HALF + HALF)
        sums = proj[yl, zz, x]
        arrived(xpart.at[half], rxr.at[half])
        for n in range(X * Y - 1):
            sums += xpart[half, n].astype(F32)
        zsum[zz] = sums
        for t in range(half * HALF, half * HALF + HALF):

            @pl.when(z != t)
            def _(t=t):
                send(zsum.at[t], zpart.at[z], 10, rzr.at[0], {"row": at_row(yl, t, x)})

    zpart[z] = zsum[z]
    arrived(zpart.at[pl.ds(0, Z - 1)], rzr.at[0])
    sums = zpart[0]
    for n in range(1, Z):
        sums += zpart[n]

    fin[me] = sums
    low = low[0:16]
    for dh, dk in PEERS:
        send(fin.at[me], fin.at[me], 11, fr.at[0], c_dev(dh, dk))
    arrived(fin.at[pl.ds(0, COLS - 1)], fr.at[0])
    for q in range(H):
        a, b = fin[2 * q], fin[2 * q + 1]
        sl = slice(q % 2 * 128, q % 2 * 128 + 128)
        out_ref[0:16, q // 2, sl] = jnp.where(low, a, pltpu.roll(b, 64, 1))
        out_ref[16:32, q // 2, sl] = jnp.where(low, pltpu.roll(a, 64, 1), b)
    arrived(col.at[pl.ds(0, 9)], sent.at[0])
    arrived(col.at[pl.ds(0, 13)], sent.at[1])
    arrived(col.at[pl.ds(0, 16)], sent.at[2])
    for n in (3, 4, 5, 6):
        arrived(col.at[pl.ds(0, 8)], sent.at[n])
    arrived(pairs, sent.at[7])
    arrived(part, sent.at[8])
    arrived(xpart, sent.at[9])
    arrived(zpart.at[pl.ds(0, Z - 1)], sent.at[10])
    arrived(fin.at[pl.ds(0, COLS - 1)], sent.at[11])


def body(orbitals, kern, basis):
    V, D = pltpu.VMEM, pltpu.SemaphoreType.DMA
    return pl.pallas_call(
        kernel,
        out_shape=jax.ShapeDtypeStruct((PIECE, 2, WIDTH // 2), F32),
        in_specs=[pl.BlockSpec(memory_space=pltpu.HBM), pl.BlockSpec(memory_space=pltpu.HBM), pl.BlockSpec(memory_space=pltpu.HBM)],
        out_specs=pl.BlockSpec(memory_space=pltpu.VMEM),
        scratch_shapes=[
            V((PIECE, 2, WIDTH // 2), BF), V((ROWS, PIECE, WIDTH), BF), V((COLS, PIECE, WIDTH), BF), V((POINTS, 2048), BF), V((POINTS, 2048), BF),
            V((1024, 512), BF), V((POINTS, WIDTH), F32), V((H, K, 128, 128), F32), V((H, 128, 128), F32), V((H, 128, 128), BF),
            V((H - 1, 128, 128), BF), V((Y, Z, X, 16, 128), F32), V((Y, Z, X, 16, 128), BF), V((2, X * Y - 1, Z // 2, 16, 128), BF),
            V((Z, 16, 128), F32), V((Z, 16, 128), F32), V((COLS, 16, 128), F32),
            D((3,)), D((12,)), D((Z,)), D((Z,)), D((Z,)), D((Z,)), D((2,)), D((Z,)), D((H,)), D((1,)), D((H,)), D((1,)), D((2,)), D((1,)), D((1,)),
        ],
        compiler_params=pltpu.CompilerParams(collective_id=0, has_side_effects=True, vmem_limit_bytes=53 << 20),
        cost_estimate=pl.CostEstimate(flops=1_300_000_000, bytes_accessed=2_300_000, transcendentals=0),
        name="exchange",
    )(orbitals, kern, basis)


def solution(mesh):
    return jax.shard_map(
        body,
        mesh=mesh,
        in_specs=(P(("row", "col"), None, None), P("row", "col"), P("row", None)),
        out_specs=P("row", None, None),
        check_vma=False,
    )
```

```python
import jax
import jax.numpy as jnp
from jax import lax
from jax.experimental import pallas as pl
from jax.experimental.pallas import tpu as pltpu
from jax.sharding import PartitionSpec as P

MESH = pl.DeviceIdType.MESH
Y, Z, X = 2, 8, 4
H, K = 4, 2
ROWS, COLS = Y * Z * X, H * K
PIECE, WIDTH = 32, 512
POINTS = COLS * PIECE
BAND = X * PIECE
HOPS = (0, 1, 7, 2, 6, 3, 5, 4)
OVER_Y = (2, 6, 3, 5, 4)
SCHEDULE = (
    "s0", "t0", "B", "s1", "s7", "c0", "Z", "s2", "s6", "c1", "s3", "s5", "R", "c7",
    "s4", "r0", "c2", "c6", "t1", "t7", "r1", "r7", "t2", "t6", "c3", "t3", "I", "n0",
    "c5", "t5", "r2", "f0", "r6", "n1", "c4", "t4", "n7", "r3", "n2", "r5", "n6", "r4",
    "f1", "f7", "n3", "n5", "f2", "n4", "f6", "f3", "f5", "f4",
)
BF, F32 = jnp.bfloat16, jnp.float32


def kernel(
    orb_ref, kernel_ref, basis_ref, out_ref,
    orb, col, rows, kern, basis, basis2, acc, packed, pairs, send16, part, proj, proj16, xpart, zsum, zpart, fin,
    load_sem, sent, zr, zr2, xr, xr3, yr, lr, hr, kr, pr, cr, rxr, rzr, fr,
):
    row, me = lax.axis_index("row"), lax.axis_index("col")
    yl, z, x = row // (Z * X), (row // X) % Z, row % X
    h, k = me // K, me % K

    def at_row(a, b, c):
        return (a * Z + b) * X + c

    def z_dev(d):
        return {"row": at_row(yl, (z + d) % Z, x)}

    def x_dev(e):
        return {"row": at_row(yl, z, (x + e) % X)}

    y_dev = {"row": at_row(1 - yl, z, x)}

    def xy_dev(n):
        return {"row": at_row((yl + n // X) % Y, z, (x + n % X) % X)}

    def c_at(dh, dk):
        return ((h + dh) % H) * K + (k + dk) % K

    def c_dev(dh, dk):
        return {"col": c_at(dh, dk)}

    PEERS = [(dh, dk) for dh in (2, 1, 3, 0) for dk in (0, 1) if (dh, dk) != (0, 0)]

    barrier = pltpu.get_barrier_semaphore()
    peers = [z_dev(d) for d in range(1, Z)] + [xy_dev(n) for n in range(1, X * Y)] + [c_dev(*p) for p in PEERS]
    for p in peers:
        pl.semaphore_signal(barrier, inc=1, device_id=p, device_id_type=MESH)

    load_o = pltpu.make_async_copy(orb_ref, orb, load_sem.at[0])
    load_k = pltpu.make_async_copy(kernel_ref, kern, load_sem.at[1])
    load_b = pltpu.make_async_copy(basis_ref, basis, load_sem.at[2])
    load_o.start()
    load_k.start()
    load_b.start()
    load_o.wait()
    for s in range(2):
        mine = orb[:, s, :]
        col[row, :, s * 256:s * 256 + 256] = mine
        rows[me, :, s * 256:s * 256 + 256] = mine
    pl.semaphore_wait(barrier, len(peers))

    def send(src, dst, group, arrival, dev):
        pltpu.make_async_remote_copy(src, dst, sent.at[group], arrival, device_id=dev, device_id_type=MESH).start()

    def arrived(like, arrival):
        pltpu.make_async_copy(like, like, arrival).wait()

    HALVES = pl.ds(0, 256), pl.ds(256, 256)
    OVER = pl.ds(0, 128), pl.ds(128, 384)

    def block(y_at, d, e=0):
        return col.at[at_row(y_at, (z - d + Z) % Z, (x - e + X) % X)]

    own = col.at[row]
    send(own, own, 0, yr.at[0], y_dev)
    for d in HOPS[1:]:
        send(own, own, 0, zr.at[d], z_dev(d))
    for dh in (2, 1, 3):
        send(rows.at[me], rows.at[me], 1, hr.at[dh], c_dev(dh, 0))
    send(rows.at[me], rows.at[me], 1, kr.at[0], c_dev(0, 1))

    def spread(d):
        b = block(yl, d)
        if d:
            arrived(b, zr.at[d])
        for e in (1, 3):
            send(b, b, 2, xr.at[d], x_dev(e))
        if d in OVER_Y:
            send(b, b, 0, yr.at[d], y_dev)

    def cross(d):
        arrived(col.at[pl.ds(0, 2)], xr.at[d])
        for n, e in enumerate((1, 3)):
            half = block(yl, d, e).at[:, HALVES[n]]
            send(half, half, 3, xr3.at[d], x_dev(e))
        for e in (1, 3):
            half = block(yl, d, e).at[:, OVER[0]]
            send(half, half, 4, lr.at[d], y_dev)

    def relay(d):
        b = block(yl, d, 2)
        arrived(b, xr3.at[d])
        send(b, b, 5, lr.at[d], y_dev)

    def fan():
        b = block(1 - yl, 0)
        for d in [d for d in HOPS[1:] if d not in OVER_Y]:
            send(b, b, 1, zr2.at[d], z_dev(d))

    def spread2(d):
        b = block(1 - yl, d)
        arrived(b, yr.at[d] if d == 0 or d in OVER_Y else zr2.at[d])
        half = b.at[:, OVER[1]]
        for e in (1, 3):
            send(half, half, 6, lr.at[d], x_dev(e))

    def last(d):
        arrived(col.at[pl.ds(0, 3)], lr.at[d])

    def rows_on():
        for dh in (1, 3, 2):
            b = rows.at[c_at(H - dh, 0)]
            arrived(b, hr.at[dh])
            send(b, b, 1, kr.at[0], c_dev(0, 1))

    def rows_in():
        arrived(rows.at[pl.ds(0, 4)], kr.at[0])
        load_k.wait()

    def prepare():
        load_b.wait()
        for half in range(2):
            t = basis[:, half * 1024:half * 1024 + 1024].T.reshape(ROWS // 2, 2, PIECE // 2, POINTS)
            for q in range(2):
                basis2[half * 512:half * 512 + 512, q * POINTS:q * POINTS + POINTS] = t[:, q].reshape(512, POINTS)

    def compute(y_at, d, first=False):
        band = y_at * Z + (z - d + Z) % Z
        c = col[pl.ds(band * X, X)].reshape(BAND, WIDTH)
        kk = kern[:, pl.ds(pl.multiple_of(band * BAND, BAND), BAND)].astype(F32)
        for s in range(2):
            sl = slice(s * 256, s * 256 + 256)
            r = rows[:, :, sl].reshape(POINTS, 256)
            den = lax.dot_general(r, c[:, sl], (((1,), (1,)), ((), ())), preferred_element_type=F32)
            w = (den * kk).astype(BF)
            t = jnp.dot(w, c[:, sl], preferred_element_type=F32)
            if first:
                acc[:, sl] = t
            else:
                acc[:, sl] += t

    started = []

    def near(d):
        compute(yl, d, not started)
        started.append(d)

    def far(d):
        last(d)
        compute(1 - yl, d)

    steps = {"s": spread, "c": cross, "r": relay, "t": spread2, "n": near, "f": far, "Z": lambda _: fan(), "R": lambda _: rows_on(), "I": lambda _: rows_in(), "B": lambda _: prepare()}
    for step in SCHEDULE:
        steps[step[0]](int(step[1:] or 0))

    low = lax.broadcasted_iota(jnp.int32, (128, 128), 1) < 64
    for q in range(H):
        top, bot = acc[0:128, q * 128:q * 128 + 128], acc[128:256, q * 128:q * 128 + 128]
        packed[q, 0] = jnp.where(low, top, pltpu.roll(bot, 64, 1))
        packed[q, 1] = jnp.where(low, pltpu.roll(top, 64, 1), bot)
    for dh in (2, 1, 3, 0):
        send(packed.at[(h + dh) % H, 1 - k], pairs.at[dh], 7, pr.at[dh], c_dev(0, 1))
    for dh in (2, 1, 3):
        arrived(pairs.at[dh], pr.at[dh])
        send16[dh] = (packed[(h + dh) % H, k] + pairs[dh]).astype(BF)
        send(send16.at[dh], part.at[dh - 1], 8, cr.at[0], c_dev(dh, 0))
    arrived(pairs.at[0], pr.at[0])
    total = packed[h, k] + pairs[0]
    arrived(part, cr.at[0])
    for n in range(H - 1):
        total += part[n].astype(F32)

    t, tr = total.astype(BF).astype(F32), pltpu.roll(total.astype(BF).astype(F32), 64, 1)
    zero = jnp.zeros_like(t)
    rhs = jnp.concatenate([jnp.where(low, t, zero), jnp.where(low, tr, zero), jnp.where(low, zero, tr), jnp.where(low, zero, t)], axis=0).astype(BF)
    HALF = Z // 2
    for half in range(2):
        zz = slice(half * HALF, half * HALF + HALF)
        for y_at in range(Y):
            r0 = (y_at * Z + half * HALF) * X * 16
            e = jnp.dot(basis2[r0:r0 + HALF * X * 16], rhs, preferred_element_type=F32).reshape(HALF, X, 16, 128)
            proj[y_at, zz] = e
            proj16[y_at, zz] = e.astype(BF)
        for n in (6, 5, 7, 2, 4, 1, 3):
            piece = proj16.at[(yl + n // X) % Y, pl.ds(half * HALF, HALF), (x + n % X) % X]
            send(piece, xpart.at[half, n - 1], 9, rxr.at[half], xy_dev(n))
    for half in range(2):
        zz = slice(half * HALF, half * HALF + HALF)
        sums = proj[yl, zz, x]
        arrived(xpart.at[half], rxr.at[half])
        for n in range(X * Y - 1):
            sums += xpart[half, n].astype(F32)
        zsum[zz] = sums
        for t in range(half * HALF, half * HALF + HALF):

            @pl.when(z != t)
            def _(t=t):
                send(zsum.at[t], zpart.at[z], 10, rzr.at[0], {"row": at_row(yl, t, x)})

    zpart[z] = zsum[z]
    arrived(zpart.at[pl.ds(0, Z - 1)], rzr.at[0])
    sums = zpart[0]
    for n in range(1, Z):
        sums += zpart[n]

    fin[me] = sums
    low = low[0:16]
    for dh, dk in PEERS:
        send(fin.at[me], fin.at[me], 11, fr.at[0], c_dev(dh, dk))
    arrived(fin.at[pl.ds(0, COLS - 1)], fr.at[0])
    for q in range(H):
        a, b = fin[2 * q], fin[2 * q + 1]
        sl = slice(q % 2 * 128, q % 2 * 128 + 128)
        out_ref[0:16, q // 2, sl] = jnp.where(low, a, pltpu.roll(b, 64, 1))
        out_ref[16:32, q // 2, sl] = jnp.where(low, pltpu.roll(a, 64, 1), b)
    arrived(col.at[pl.ds(0, Z + len(OVER_Y))], sent.at[0])
    arrived(col.at[pl.ds(0, 14 - len(OVER_Y))], sent.at[1])
    arrived(col.at[pl.ds(0, 16)], sent.at[2])
    for n, blocks in enumerate((8, 4, 8, 12)):
        arrived(col.at[pl.ds(0, blocks)], sent.at[3 + n])
    arrived(pairs, sent.at[7])
    arrived(part, sent.at[8])
    arrived(xpart, sent.at[9])
    arrived(zpart.at[pl.ds(0, Z - 1)], sent.at[10])
    arrived(fin.at[pl.ds(0, COLS - 1)], sent.at[11])


def body(orbitals, kern, basis):
    V, D = pltpu.VMEM, pltpu.SemaphoreType.DMA
    return pl.pallas_call(
        kernel,
        out_shape=jax.ShapeDtypeStruct((PIECE, 2, WIDTH // 2), F32),
        in_specs=[pl.BlockSpec(memory_space=pltpu.HBM), pl.BlockSpec(memory_space=pltpu.HBM), pl.BlockSpec(memory_space=pltpu.HBM)],
        out_specs=pl.BlockSpec(memory_space=pltpu.VMEM),
        scratch_shapes=[
            V((PIECE, 2, WIDTH // 2), BF), V((ROWS, PIECE, WIDTH), BF), V((COLS, PIECE, WIDTH), BF), V((POINTS, 2048), BF), V((POINTS, 2048), BF),
            V((1024, 512), BF), V((POINTS, WIDTH), F32), V((H, K, 128, 128), F32), V((H, 128, 128), F32), V((H, 128, 128), BF),
            V((H - 1, 128, 128), BF), V((Y, Z, X, 16, 128), F32), V((Y, Z, X, 16, 128), BF), V((2, X * Y - 1, Z // 2, 16, 128), BF),
            V((Z, 16, 128), F32), V((Z, 16, 128), F32), V((COLS, 16, 128), F32),
            D((3,)), D((12,)), D((Z,)), D((Z,)), D((Z,)), D((Z,)), D((Z,)), D((Z,)), D((H,)), D((1,)), D((H,)), D((1,)), D((2,)), D((1,)), D((1,)),
        ],
        compiler_params=pltpu.CompilerParams(collective_id=0, has_side_effects=True, vmem_limit_bytes=53 << 20),
        cost_estimate=pl.CostEstimate(flops=1_300_000_000, bytes_accessed=2_300_000, transcendentals=0),
        name="exchange",
    )(orbitals, kern, basis)


def solution(mesh):
    return jax.shard_map(
        body,
        mesh=mesh,
        in_specs=(P(("row", "col"), None, None), P("row", "col"), P("row", None)),
        out_specs=P("row", None, None),
        check_vma=False,
    )
```
